512 devices in a mesh: gx: 64 (over z, y), gy: 8 (over x, core).
Axes of the slice: x: 4, y: 4, z: 16, core: 2. Of those that a mesh axis runs over, the one named last changes fastest.
Arguments:
- volume: bfloat16 [128, 64, 4096], P('gx', 'gy'), may hold values from -130 to 130
- conv_first: bfloat16 [1728, 64], replicated, may hold values from -0.96225045 to 0.96225045
- gain: float32 [64], replicated, may hold values from 0.5 to 1.5
- shift: float32 [64], replicated, may hold values from -3 to 3
- conv_second: bfloat16 [1728, 64], replicated, may hold values from -0.15625 to 0.15625
- bias_second: float32 [64], replicated, may hold values from -3 to 3
Outputs:
- result: bfloat16 [128, 64, 4096], P('gx', 'gy')
The draws below stay inside these ranges and needn't reach their ends.
All inputs are finite; a program needn't handle non-finite values.
Results may differ from the reference program's by a relative error of at most 0.004.
Values may be sent and summed in bfloat16 or wider, within the bound.
No kernel may reach another device: no remote copies, remote signals or barrier semaphores. Data moves between devices by JAX's collectives and lax.ppermute only.
A program may use at most 64 MiB of HBM per device.

```python
import math
import jax
import jax.numpy as jnp
from jax import lax

C = 64
CX = 2
CY = 8
Z = 64
NEWTON = 5
NX = 128
NY = 64


def draw_volume(key, part):
    key_base = jax.random.fold_in(key, 21)
    key_scale = jax.random.fold_in(key, 22)
    key_offset = jax.random.fold_in(key, 23)
    key_heavy_x = jax.random.fold_in(key, 26)
    key_heavy_y = jax.random.fold_in(key, 27)
    x_block = jnp.arange(NX, dtype=jnp.int32) * 5 // NX
    y_block = jnp.arange(NY, dtype=jnp.int32) * 3 // NY
    table_scale = jnp.exp(jax.random.uniform(key_scale, (5, 3, C), jnp.float32, -1.0, 1.0))
    table_offset = jax.random.uniform(key_offset, (5, 3, C), jnp.float32, -1.0, 1.0)
    cell_scale = table_scale[x_block[:, None], y_block[None, :]]
    cell_offset = table_offset[x_block[:, None], y_block[None, :]]
    x_ramp = 0.5 + (jnp.arange(NX, dtype=jnp.float32) + 0.5) / NX
    heavy_x = jax.random.randint(key_heavy_x, (), 0, NX // CX)
    heavy_y = jax.random.randint(key_heavy_y, (), 0, NY // CY)
    in_x = jnp.arange(NX, dtype=jnp.int32) // CX == heavy_x
    in_y = jnp.arange(NY, dtype=jnp.int32) // CY == heavy_y
    heavy = 1.0 + 9.0 * (in_x[:, None] & in_y[None, :]).astype(jnp.float32)
    base = jnp.clip(jax.random.normal(key_base, (NX, NY, Z, C), jnp.float32), -3.0, 3.0)
    factor = x_ramp[:, None, None, None] * cell_scale[:, :, None, :] * heavy[:, :, None, None]
    full = base * factor + cell_offset[:, :, None, :]
    return full.reshape(NX, NY, Z * C).astype(jnp.bfloat16)


def draw_conv_first(key, part):
    key_base = jax.random.fold_in(key, 11)
    key_scale = jax.random.fold_in(key, 12)
    scales = jnp.exp(jax.random.uniform(key_scale, (C,), jnp.float32, 0.0, math.log(10.0)))
    base = jnp.clip(jax.random.normal(key_base, (27 * C, C), jnp.float32), -4.0, 4.0)
    return (base * scales[None, :] / jnp.sqrt(jnp.float32(27 * C))).astype(jnp.bfloat16)


def noise(key, shape, spread, limit, held_as=jnp.bfloat16):
    entries = spread * jax.random.normal(key, shape, jnp.float32)
    return jnp.clip(entries, min=-limit, max=limit).astype(held_as)


def setup_inputs(seed: int = 0) -> dict:
    key_of = jax.random.split(jax.random.key(seed), 7)
    volume = draw_volume(jax.random.fold_in(key_of[6], 71), 0)
    conv_first = draw_conv_first(jax.random.fold_in(key_of[6], 71), 0)
    gain = jnp.clip(jax.random.uniform(key_of[2], (C,), jnp.float32, 0.5, 1.5), 0.5, 1.5)
    shift = noise(key_of[3], (C,), 0.5, 3.0, jnp.float32)
    conv_second = noise(key_of[4], (27 * C, C), (27 * C) ** -0.5, 0.15625)
    bias_second = noise(key_of[5], (C,), 0.5, 3.0, jnp.float32)
    return dict(volume=volume, conv_first=conv_first, gain=gain, shift=shift, conv_second=conv_second, bias_second=bias_second)


def conv(vol, weights):
    nx, ny, z, c = vol.shape
    padded = jnp.pad(vol, ((1, 1), (1, 1), (1, 1), (0, 0)))
    zcat = jnp.concatenate([padded[:, :, 0:z], padded[:, :, 1:z + 1], padded[:, :, 2:z + 2]], axis=3)
    acc = jnp.zeros((nx * ny * z, c), jnp.float32)
    for dx in range(3):
        for dy in range(3):
            tap = zcat[dx:dx + nx, dy:dy + ny].reshape(-1, 3 * c)
            first = (dx * 3 + dy) * 3 * c
            acc = acc + jnp.dot(tap, weights[first:first + 3 * c], preferred_element_type=jnp.float32)
    return acc

def newton_whiten(sigma):
    dims = sigma.shape[0]
    trace_value = jnp.trace(sigma)
    normed = sigma / trace_value
    proj = jnp.eye(dims, dtype=jnp.float32)
    for step in range(NEWTON):
        cube = jnp.dot(jnp.dot(proj, proj, precision=lax.Precision.HIGHEST), proj, precision=lax.Precision.HIGHEST)
        proj = 1.5 * proj - 0.5 * jnp.dot(cube, normed, precision=lax.Precision.HIGHEST)
    return proj / jnp.sqrt(trace_value)

def reference(volume, conv_first, gain, shift, conv_second, bias_second):
    vol = volume.reshape(NX, NY, Z, C)
    hidden = conv(vol, conv_first)
    count = float(NX * NY * Z)
    mean = lax.optimization_barrier(jnp.sum(hidden, axis=0)) / count
    centered = hidden - mean[None, :]
    sigma = jnp.dot(centered.T, centered, precision=lax.Precision.HIGHEST) / count + 1e-05 * jnp.eye(C, dtype=jnp.float32)
    whiten = newton_whiten(sigma)
    normalized = jnp.dot(centered, whiten, precision=lax.Precision.HIGHEST)
    act = jnp.maximum(gain[None, :] * normalized + shift[None, :], 0.0).astype(jnp.bfloat16)
    out = conv(act.reshape(NX, NY, Z, C), conv_second) + bias_second[None, :]
    return out.astype(jnp.bfloat16).reshape(NX, NY, Z * C)
```

```python
import functools

import jax
import jax.numpy as jnp
from jax import lax
from jax.sharding import Mesh
from jax.sharding import PartitionSpec as P

NEWTON = 5
GX = ("gx_0", "gx_1")
GY = ("gy_0", "gy_1")


def padded_2(block, sides, width):
    for axis, dim in sides:
        count = lax.axis_size(axis)
        forward = [(i, i + 1) for i in range(count - 1)]
        backward = [(target, source) for source, target in forward]
        low = lax.ppermute(
            lax.slice_in_dim(block, block.shape[dim] - width, None, axis=dim), axis, forward
        )
        high = lax.ppermute(lax.slice_in_dim(block, 0, width, axis=dim), axis, backward)
        block = jnp.concatenate([low, block, high], axis=dim)
    return block


def convolve(padded, weights, depth):
    width = weights.shape[1]
    rows_x = padded.shape[0] - 2
    rows_y = padded.shape[1] - 2
    vol = padded.reshape(rows_x + 2, rows_y + 2, depth, width)
    zpad = jnp.pad(vol, ((0, 0), (0, 0), (1, 1), (0, 0)))
    zcat = jnp.concatenate(
        [zpad[:, :, 0:depth], zpad[:, :, 1 : depth + 1], zpad[:, :, 2 : depth + 2]], axis=3
    )
    acc = jnp.zeros((rows_x * rows_y * depth, width), jnp.float32)
    for dx in range(3):
        for dy in range(3):
            tap = zcat[dx : dx + rows_x, dy : dy + rows_y].reshape(-1, 3 * width)
            first = (dx * 3 + dy) * 3 * width
            acc = acc + jnp.dot(
                tap, weights[first : first + 3 * width], preferred_element_type=jnp.float32
            )
    return acc


def newton_whiten(sigma):
    dims = sigma.shape[0]
    trace_value = jnp.trace(sigma)
    normed = sigma / trace_value
    proj = jnp.eye(dims, dtype=jnp.float32)
    for step in range(NEWTON):
        cube = jnp.dot(
            jnp.dot(proj, proj, precision=lax.Precision.HIGHEST),
            proj,
            precision=lax.Precision.HIGHEST,
        )
        proj = 1.5 * proj - 0.5 * jnp.dot(cube, normed, precision=lax.Precision.HIGHEST)
    return proj / jnp.sqrt(trace_value)


def exchange_sum(block, axes):
    count = functools.reduce(lambda total, axis: total * lax.axis_size(axis), axes, 1)
    copies = jnp.broadcast_to(block[None], (count,) + block.shape)
    return jnp.sum(lax.all_to_all(copies, axes, 0, 0, tiled=True), axis=0)


def total_over_mesh(local_sum, local_gram):
    width = local_sum.shape[0]
    row = jnp.concatenate([local_sum, jnp.zeros_like(local_sum)])
    packed = jnp.concatenate([local_gram.reshape(-1, 1, 2 * width), row.reshape(1, 1, 2 * width)], axis=0)
    total = exchange_sum(exchange_sum(packed, GX[:1]), GX[1:] + GY)
    return total[-1, 0, :width], total[:-1].reshape(width, width)


def statistics(hidden, count):
    width = hidden.shape[1]
    ident = jnp.eye(width, dtype=jnp.float32)
    local_sum = jnp.sum(hidden, axis=0)
    local_gram = jnp.dot(hidden.T, hidden, precision=lax.Precision.HIGHEST)
    total_sum, total_gram = total_over_mesh(local_sum, local_gram)
    mean = total_sum / count
    sigma = total_gram / count - mean[:, None] * mean[None, :] + 1e-05 * ident
    return (mean, newton_whiten(sigma))


def activate(hidden, mean, whiten, gain, shift):
    normalized = jnp.dot(hidden - mean[None, :], whiten, precision=lax.Precision.HIGHEST)
    return jnp.maximum(gain[None, :] * normalized + shift[None, :], 0.0)


def inside_grid(rows_x, rows_y):
    pos_x = lax.axis_index(GX) * rows_x + jnp.arange(rows_x + 2, dtype=jnp.int32) - 1
    pos_y = lax.axis_index(GY) * rows_y + jnp.arange(rows_y + 2, dtype=jnp.int32) - 1
    inside_x = ((pos_x >= 0) & (pos_x < rows_x * lax.axis_size(GX))).astype(jnp.float32)
    inside_y = ((pos_y >= 0) & (pos_y < rows_y * lax.axis_size(GY))).astype(jnp.float32)
    return (inside_x[:, None] * inside_y[None, :]).reshape(rows_x + 2, rows_y + 2, 1, 1)


def rimmed_act(rimmed_rows, mean, whiten, gain, shift, rows_x, rows_y, depth):
    width = mean.shape[0]
    act = activate(rimmed_rows, mean, whiten, gain, shift)
    act = act.reshape(rows_x + 2, rows_y + 2, depth, width) * inside_grid(rows_x, rows_y)
    return act.astype(jnp.bfloat16).reshape(rows_x + 2, rows_y + 2, depth * width)


def local(volume, conv_first, gain, shift, conv_second, bias_second):
    width = bias_second.shape[0]
    rows_x, rows_y, merged = volume.shape
    depth = merged // width
    count = float(rows_x * lax.axis_size(GX) * rows_y * lax.axis_size(GY) * depth)
    rim_depth = 2
    padded = padded_2(volume, ((GX, 0), (GY, 1)), rim_depth)
    hidden_all = convolve(padded, conv_first, depth)
    widened = hidden_all.reshape(rows_x + 2, rows_y + 2, depth, width)
    hidden = widened[1:-1, 1:-1].reshape(-1, width)
    mean, whiten = statistics(hidden, count)
    act_padded = rimmed_act(hidden_all, mean, whiten, gain, shift, rows_x, rows_y, depth)
    out = convolve(act_padded, conv_second, depth) + bias_second[None, :]
    return out.astype(jnp.bfloat16).reshape(rows_x, rows_y, merged)


def solution(mesh):
    torus = Mesh(mesh.devices.reshape(16, 4, 4, 2), ("gx_0", "gx_1", "gy_0", "gy_1"))
    placed = (P(GX, GY, None), P(), P(), P(), P(), P())
    return jax.shard_map(
        local, mesh=torus, in_specs=placed, out_specs=P(GX, GY, None), check_vma=False
    )
```

```python
import functools

import jax
import jax.numpy as jnp
from jax import lax
from jax.experimental import pallas as pl
from jax.experimental.pallas import tpu as pltpu
from jax.sharding import Mesh
from jax.sharding import PartitionSpec as P

NEWTON = 5
GX = ("gx_0", "gx_1")
GY = ("gy_0", "gy_1")
PACK = 4
F32 = jnp.float32
BF16 = jnp.bfloat16
HIGHEST = lax.Precision.HIGHEST
PAY = 17


def params():
    return pltpu.CompilerParams(vmem_limit_bytes=48 * 1024 * 1024)


def shift_exchange(low_edge, high_edge, axis):
    count = lax.axis_size(axis)
    forward = [(i, i + 1) for i in range(count - 1)]
    backward = [(target, source) for source, target in forward]
    return lax.ppermute(high_edge, axis, forward), lax.ppermute(low_edge, axis, backward)


def rows_kernel(v_ref, o_ref, f_ref):
    slabs, sub, merged = v_ref.shape
    rows, lanes = o_ref.shape[2:]
    for x in range(slabs):
        for b in range(rows):
            for h in range(lanes // 128):
                first = b * lanes + h * 128
                f_ref[h, pl.ds(x * sub * rows + b, sub, stride=rows), :] = v_ref[
                    x, :, first : first + 128
                ].astype(F32)
    for h in range(lanes // 128):
        o_ref[:, :, :, h * 128 : (h + 1) * 128] = f_ref[h].astype(BF16).reshape(slabs, sub, rows, 128)


def band_kernel(w_ref, o_ref):
    c = w_ref.shape[0]
    o_ref[...] = jnp.zeros_like(o_ref)
    for t in range(9):
        w = w_ref[:, t * 3 * c : (t + 1) * 3 * c]
        base = t * 6 * c
        o_ref[0:c, base : base + 2 * c] = w[:, c:]
        o_ref[0:c, base + 5 * c : base + 6 * c] = w[:, :c]
        for k in range(1, PACK):
            first = base + (k - 1) * c
            o_ref[k * c : (k + 1) * c, first : first + 3 * c] = w


def widen(f_ref, x_ref):
    rows = x_ref.shape[2]
    x_ref[:, :, :, 0:256] = f_ref[:, :, 8 : 8 + rows, :].astype(BF16)
    after = f_ref[:, :, 9 : 9 + rows, 0:128]
    before = f_ref[:, :, 7 : 7 + rows, 128:256]
    lane = lax.broadcasted_iota(jnp.int32, after.shape, 3)
    x_ref[:, :, :, 256:384] = jnp.where(lane < 64, after, before).astype(BF16)


def clear_ends(f_ref, rows):
    cells_x, cells_y, _, lanes = f_ref.shape
    zero = jnp.zeros((cells_x, cells_y, 8, lanes), F32)
    f_ref[:, :, 0:8, :] = zero
    f_ref[:, :, 8 + rows : 16 + rows, :] = zero


def banded_conv(x_ref, w_ref):
    nx, ny, rows, k = x_ref.shape
    nx, ny = nx - 2, ny - 2
    acc = None
    for dx in range(3):
        taps = [x_ref[dx : dx + nx, dy : dy + ny].reshape(nx * ny * rows, k) for dy in range(3)]
        part = lax.dot_general(
            jnp.concatenate(taps, axis=1),
            w_ref[:, dx * 3 * k : (dx + 1) * 3 * k],
            (((1,), (1,)), ((), ())),
            preferred_element_type=F32,
        )
        acc = part if acc is None else acc + part
    return acc


def square_iota(n):
    return lax.broadcasted_iota(jnp.int32, (n, n), 0), lax.broadcasted_iota(jnp.int32, (n, n), 1)


def hidden_kernel(own_ref, xlo_ref, xhi_ref, ylo_ref, yhi_ref, w_ref, hidden_ref, pay_ref, f_ref, x_ref):
    rows = own_ref.shape[2]
    cx, cy = own_ref.shape[:2]
    clear_ends(f_ref, rows)
    f_ref[:, 0:2, 8 : 8 + rows, :] = ylo_ref[...].astype(F32)
    f_ref[0:2, 2 : 2 + cy, 8 : 8 + rows, :] = xlo_ref[...].astype(F32)
    f_ref[2 : 2 + cx, 2 : 2 + cy, 8 : 8 + rows, :] = own_ref[...].astype(F32)
    f_ref[2 + cx : 4 + cx, 2 : 2 + cy, 8 : 8 + rows, :] = xhi_ref[...].astype(F32)
    f_ref[:, 2 + cy : 4 + cy, 8 : 8 + rows, :] = yhi_ref[...].astype(F32)
    widen(f_ref, x_ref)
    hidden_ref[...] = banded_conv(x_ref, w_ref).reshape(hidden_ref.shape)
    own = hidden_ref[1 : 1 + cx, 1 : 1 + cy].reshape(cx * cy * rows, 256)
    wide = lax.dot_general(own, own, (((0,), (0,)), ((), ())), precision=HIGHEST, preferred_element_type=F32)
    sums = jnp.sum(own, axis=0, keepdims=True)
    gram = wide[0:64, 0:64]
    total = sums[:, 0:64]
    for k in range(1, PACK):
        gram = gram + wide[k * 64 : (k + 1) * 64, k * 64 : (k + 1) * 64]
        total = total + sums[:, k * 64 : (k + 1) * 64]
    i, j = square_iota(32)
    low = gram[32:, 32:]
    tri = jnp.where(j >= i, gram[:32, :32], low)
    cross = gram[:32, 32:]
    block = jnp.concatenate([tri[:16], tri[16:], cross[:16], cross[16:]], axis=1)
    diag = jnp.sum(jnp.where(i == j, low, 0.0), axis=0, keepdims=True)
    last = jnp.concatenate([diag, total, jnp.zeros((1, 32), F32)], axis=1)
    for p in range(pay_ref.shape[0]):
        for r in range(16):
            pay_ref[p, r] = block[r : r + 1]
        pay_ref[p, 16] = last


def relay_kernel(in_ref, out_ref):
    total = jnp.sum(in_ref[...], axis=0)
    for p in range(out_ref.shape[0]):
        out_ref[p] = total


def transposed(a):
    return jnp.transpose(a)


def moments(pay_ref, p_ref, count):
    total = jnp.sum(pay_ref[...], axis=0)
    for r in range(PAY):
        p_ref[r : r + 1, :] = total[r]
    block = p_ref[0:16, :]
    last = p_ref[16:17, :]
    i, j = square_iota(32)
    tri = jnp.concatenate([block[:, 0:32], block[:, 32:64]], axis=0)
    cross = jnp.concatenate([block[:, 64:96], block[:, 96:128]], axis=0)
    flip = transposed(tri)
    top = jnp.where(j >= i, tri, flip)
    low = jnp.where(j < i, tri, flip)
    low = jnp.where(i == j, jnp.broadcast_to(last[:, 0:32], (32, 32)), low)
    gram = jnp.concatenate(
        [
            jnp.concatenate([top, cross], axis=1),
            jnp.concatenate([transposed(cross), low], axis=1),
        ],
        axis=0,
    )
    mean = last[:, 32:96] / count
    i, j = square_iota(64)
    eye = jnp.where(i == j, 1.0, 0.0).astype(F32)
    column = jnp.sum(eye * mean, axis=1, keepdims=True)
    return mean, gram / count - column * mean + 1e-05 * eye, eye


def newton_whiten(sigma, eye):
    dot = functools.partial(jnp.dot, precision=HIGHEST, preferred_element_type=F32)
    trace = jnp.sum(jnp.sum(sigma * eye, axis=1, keepdims=True), axis=0, keepdims=True)
    normed = sigma / trace
    proj = 1.5 * eye - 0.5 * normed
    for _ in range(NEWTON - 1):
        both = dot(proj, jnp.concatenate([proj, normed], axis=1))
        proj = 1.5 * proj - 0.5 * dot(both[:, 0:64], both[:, 64:128])
    return proj / jnp.sqrt(trace)


def output_kernel(
    inside_ref, pay_ref, hidden_ref, gain_ref, shift_ref, w_ref, bias_ref, out_ref, p_ref, f_ref, x_ref, o_ref, *, count
):
    nx, ny, rows, lanes = hidden_ref.shape
    mean, sigma, eye = moments(pay_ref, p_ref, count)
    whiten = newton_whiten(sigma, eye)
    i, j = square_iota(lanes)
    wide = jnp.concatenate([whiten] * PACK, axis=1)
    wide = jnp.concatenate([wide] * PACK, axis=0)
    wide = jnp.where(i >> 6 == j >> 6, wide, 0.0)
    mean = jnp.concatenate([mean] * PACK, axis=1)
    gain = jnp.concatenate([gain_ref[...]] * PACK, axis=1)
    shift = jnp.concatenate([shift_ref[...]] * PACK, axis=1)
    centered = hidden_ref[...].reshape(nx * ny * rows, lanes) - mean
    normalized = jnp.dot(centered, wide, precision=HIGHEST, preferred_element_type=F32)
    act = jnp.maximum(gain * normalized + shift, 0.0).reshape(hidden_ref.shape)
    clear_ends(f_ref, rows)
    f_ref[:, :, 8 : 8 + rows, :] = act
    for flag, edge in ((0, f_ref.at[0]), (1, f_ref.at[nx - 1]), (2, f_ref.at[:, 0]), (3, f_ref.at[:, ny - 1])):

        @pl.when(inside_ref[flag] == 0)
        def _(edge=edge):
            edge[...] = jnp.zeros_like(edge)

    widen(f_ref, x_ref)
    bias = jnp.concatenate([bias_ref[...]] * PACK, axis=1)
    result = banded_conv(x_ref, w_ref) + bias
    for h in range(lanes // 128):
        o_ref[h] = result[:, h * 128 : (h + 1) * 128]
    slabs, sub, _ = out_ref.shape
    for x in range(slabs):
        for b in range(rows):
            for h in range(lanes // 128):
                first = b * lanes + h * 128
                out_ref[x, :, first : first + 128] = o_ref[
                    h, pl.ds(x * sub * rows + b, sub, stride=rows), :
                ].astype(BF16)


def exchange(block, axes):
    return lax.all_to_all(block, axes, 0, 0, tiled=True)


def group_size(axes):
    return functools.reduce(lambda total, axis: total * lax.axis_size(axis), axes, 1)


def local(volume, conv_first, gain, shift, conv_second, bias_second):
    width = bias_second.shape[0]
    cx, cy, merged = volume.shape
    lanes = PACK * width
    rows = merged // lanes
    count = float(cx * group_size(GX) * cy * group_size(GY) * (merged // width))
    call = functools.partial(pl.pallas_call, compiler_params=params())
    own = call(
        rows_kernel,
        out_shape=jax.ShapeDtypeStruct((cx, cy, rows, lanes), BF16),
        scratch_shapes=[pltpu.VMEM((lanes // 128, cx * cy * rows, 128), F32)],
        name="rows",
    )(volume)
    band = call(band_kernel, out_shape=jax.ShapeDtypeStruct((lanes, 54 * width), BF16), name="band")
    first, second = band(conv_first.T), band(conv_second.T)
    xlo, xhi = shift_exchange(own[:2], own[cx - 2 :], GX)
    sides = jnp.concatenate([xlo, own, xhi], axis=0)
    ylo, yhi = shift_exchange(sides[:, :2], sides[:, cy - 2 :], GY)
    hidden, pay = call(
        hidden_kernel,
        out_shape=(
            jax.ShapeDtypeStruct((cx + 2, cy + 2, rows, lanes), F32),
            jax.ShapeDtypeStruct((group_size(GX[:1]), PAY, 1, 128), F32),
        ),
        scratch_shapes=[
            pltpu.VMEM((cx + 4, cy + 4, rows + 16, lanes), F32),
            pltpu.VMEM((cx + 4, cy + 4, rows, 6 * width), BF16),
        ],
        name="hidden",
    )(own, xlo, xhi, ylo, yhi, first)
    rest = GX[1:] + GY
    pay = exchange(pay, GX[:1])
    pay = call(
        relay_kernel, out_shape=jax.ShapeDtypeStruct((group_size(rest), PAY, 1, 128), F32), name="relay"
    )(pay)
    pay = exchange(pay, rest)
    at_x, at_y = lax.axis_index(GX), lax.axis_index(GY)
    inside = jnp.stack([at_x > 0, at_x < group_size(GX) - 1, at_y > 0, at_y < group_size(GY) - 1]).astype(jnp.int32)
    in_vmem = pl.BlockSpec(memory_space=pltpu.VMEM)
    return call(
        functools.partial(output_kernel, count=count),
        out_shape=jax.ShapeDtypeStruct((cx, cy, merged), BF16),
        in_specs=[pl.BlockSpec(memory_space=pltpu.SMEM)] + [in_vmem] * 6,
        out_specs=in_vmem,
        scratch_shapes=[
            pltpu.VMEM((24, 128), F32),
            pltpu.VMEM((cx + 2, cy + 2, rows + 16, lanes), F32),
            pltpu.VMEM((cx + 2, cy + 2, rows, 6 * width), BF16),
            pltpu.VMEM((lanes // 128, cx * cy * rows, 128), F32),
        ],
        name="output",
    )(inside, pay, hidden, gain[None], shift[None], second, bias_second[None])


def solution(mesh):
    torus = Mesh(mesh.devices.reshape(16, 4, 4, 2), GX + GY)
    placed = (P(GX, GY, None), P(), P(), P(), P(), P())
    return jax.shard_map(
        local, mesh=torus, in_specs=placed, out_specs=P(GX, GY, None), check_vma=False
    )
```

```python
import functools

import jax
import jax.numpy as jnp
from jax import lax
from jax.experimental import pallas as pl
from jax.experimental.pallas import tpu as pltpu
from jax.sharding import Mesh
from jax.sharding import PartitionSpec as P

NEWTON = 5
GX = ("gx_0", "gx_1")
GY = ("gy_0", "gy_1")
PACK = 4
F32 = jnp.float32
BF16 = jnp.bfloat16
HIGHEST = lax.Precision.HIGHEST
PAY = 17


def params():
    return pltpu.CompilerParams(vmem_limit_bytes=48 * 1024 * 1024)


def shift_exchange(low_edge, high_edge, axis):
    count = lax.axis_size(axis)
    forward = [(i, i + 1) for i in range(count - 1)]
    backward = [(target, source) for source, target in forward]
    return lax.ppermute(high_edge, axis, forward), lax.ppermute(low_edge, axis, backward)


def rows_kernel(v_ref, o_ref, f_ref):
    slabs, sub, merged = v_ref.shape
    rows, lanes = o_ref.shape[2:]
    for x in range(slabs):
        for b in range(rows):
            for h in range(lanes // 128):
                first = b * lanes + h * 128
                f_ref[h, pl.ds(x * sub * rows + b, sub, stride=rows), :] = v_ref[
                    x, :, first : first + 128
                ].astype(F32)
    for h in range(lanes // 128):
        o_ref[:, :, :, h * 128 : (h + 1) * 128] = f_ref[h].astype(BF16).reshape(slabs, sub, rows, 128)


def band_kernel(w_ref, o_ref):
    c = w_ref.shape[0]
    o_ref[...] = jnp.zeros_like(o_ref)
    for t in range(9):
        w = w_ref[:, t * 3 * c : (t + 1) * 3 * c]
        base = t * 6 * c
        o_ref[0:c, base : base + 2 * c] = w[:, c:]
        o_ref[0:c, base + 5 * c : base + 6 * c] = w[:, :c]
        for k in range(1, PACK):
            first = base + (k - 1) * c
            o_ref[k * c : (k + 1) * c, first : first + 3 * c] = w


def widen(f_ref, x_ref):
    rows = x_ref.shape[2]
    x_ref[:, :, :, 0:256] = f_ref[:, :, 8 : 8 + rows, :].astype(BF16)
    after = f_ref[:, :, 9 : 9 + rows, 0:128]
    before = f_ref[:, :, 7 : 7 + rows, 128:256]
    lane = lax.broadcasted_iota(jnp.int32, after.shape, 3)
    x_ref[:, :, :, 256:384] = jnp.where(lane < 64, after, before).astype(BF16)


def clear_ends(f_ref, rows):
    cells_x, cells_y, _, lanes = f_ref.shape
    zero = jnp.zeros((cells_x, cells_y, 8, lanes), F32)
    f_ref[:, :, 0:8, :] = zero
    f_ref[:, :, 8 + rows : 16 + rows, :] = zero


def banded_conv(x_ref, w_ref):
    nx, ny, rows, k = x_ref.shape
    nx, ny = nx - 2, ny - 2
    acc = None
    for dx in range(3):
        taps = [x_ref[dx : dx + nx, dy : dy + ny].reshape(nx * ny * rows, k) for dy in range(3)]
        part = lax.dot_general(
            jnp.concatenate(taps, axis=1),
            w_ref[:, dx * 3 * k : (dx + 1) * 3 * k],
            (((1,), (1,)), ((), ())),
            preferred_element_type=F32,
        )
        acc = part if acc is None else acc + part
    return acc


def square_iota(n):
    return lax.broadcasted_iota(jnp.int32, (n, n), 0), lax.broadcasted_iota(jnp.int32, (n, n), 1)


def hidden_kernel(own_ref, xlo_ref, xhi_ref, ylo_ref, yhi_ref, w_ref, hidden_ref, pay_ref, f_ref, x_ref):
    rows = own_ref.shape[2]
    cx, cy = own_ref.shape[:2]
    clear_ends(f_ref, rows)
    f_ref[:, 0:2, 8 : 8 + rows, :] = ylo_ref[...].astype(F32)
    f_ref[0:2, 2 : 2 + cy, 8 : 8 + rows, :] = xlo_ref[...].astype(F32)
    f_ref[2 : 2 + cx, 2 : 2 + cy, 8 : 8 + rows, :] = own_ref[...].astype(F32)
    f_ref[2 + cx : 4 + cx, 2 : 2 + cy, 8 : 8 + rows, :] = xhi_ref[...].astype(F32)
    f_ref[:, 2 + cy : 4 + cy, 8 : 8 + rows, :] = yhi_ref[...].astype(F32)
    widen(f_ref, x_ref)
    hidden_ref[...] = banded_conv(x_ref, w_ref).reshape(hidden_ref.shape)
    own = hidden_ref[1 : 1 + cx, 1 : 1 + cy].reshape(cx * cy * rows, 256)
    wide = lax.dot_general(own, own, (((0,), (0,)), ((), ())), precision=HIGHEST, preferred_element_type=F32)
    sums = jnp.sum(own, axis=0, keepdims=True)
    gram = wide[0:64, 0:64]
    total = sums[:, 0:64]
    for k in range(1, PACK):
        gram = gram + wide[k * 64 : (k + 1) * 64, k * 64 : (k + 1) * 64]
        total = total + sums[:, k * 64 : (k + 1) * 64]
    i, j = square_iota(32)
    low = gram[32:, 32:]
    tri = jnp.where(j >= i, gram[:32, :32], low)
    cross = gram[:32, 32:]
    block = jnp.concatenate([tri[:16], tri[16:], cross[:16], cross[16:]], axis=1)
    diag = jnp.sum(jnp.where(i == j, low, 0.0), axis=0, keepdims=True)
    last = jnp.concatenate([diag, total, jnp.zeros((1, 32), F32)], axis=1)
    for p in range(pay_ref.shape[0]):
        for r in range(16):
            pay_ref[p, r] = block[r : r + 1]
        pay_ref[p, 16] = last


def relay_kernel(in_ref, out_ref):
    total = jnp.sum(in_ref[...], axis=0)
    for p in range(out_ref.shape[0]):
        out_ref[p] = total


def transposed(a):
    return jnp.transpose(a)


def moments(pay_ref, p_ref, count):
    total = jnp.sum(pay_ref[...], axis=0)
    for r in range(PAY):
        p_ref[r : r + 1, :] = total[r]
    block = p_ref[0:16, :]
    last = p_ref[16:17, :]
    i, j = square_iota(32)
    tri = jnp.concatenate([block[:, 0:32], block[:, 32:64]], axis=0)
    cross = jnp.concatenate([block[:, 64:96], block[:, 96:128]], axis=0)
    flip = transposed(tri)
    top = jnp.where(j >= i, tri, flip)
    low = jnp.where(j < i, tri, flip)
    low = jnp.where(i == j, jnp.broadcast_to(last[:, 0:32], (32, 32)), low)
    gram = jnp.concatenate(
        [
            jnp.concatenate([top, cross], axis=1),
            jnp.concatenate([transposed(cross), low], axis=1),
        ],
        axis=0,
    )
    mean = last[:, 32:96] / count
    i, j = square_iota(64)
    eye = jnp.where(i == j, 1.0, 0.0).astype(F32)
    column = jnp.sum(eye * mean, axis=1, keepdims=True)
    return mean, gram / count - column * mean + 1e-05 * eye, eye


def newton_whiten(sigma, eye):
    dot = functools.partial(jnp.dot, precision=HIGHEST, preferred_element_type=F32)
    trace = jnp.sum(jnp.sum(sigma * eye, axis=1, keepdims=True), axis=0, keepdims=True)
    normed = sigma / trace
    proj = 1.5 * eye - 0.5 * normed
    for _ in range(NEWTON - 1):
        both = dot(proj, jnp.concatenate([proj, normed], axis=1))
        proj = 1.5 * proj - 0.5 * dot(both[:, 0:64], both[:, 64:128])
    return proj / jnp.sqrt(trace)


def output_kernel(
    inside_ref, pay_ref, hidden_ref, gain_ref, shift_ref, w_ref, bias_ref, out_ref, p_ref, f_ref, x_ref, o_ref, *, count
):
    nx, ny, rows, lanes = hidden_ref.shape
    mean, sigma, eye = moments(pay_ref, p_ref, count)
    whiten = newton_whiten(sigma, eye)
    i, j = square_iota(lanes)
    wide = jnp.concatenate([whiten] * PACK, axis=1)
    wide = jnp.concatenate([wide] * PACK, axis=0)
    wide = jnp.where(i >> 6 == j >> 6, wide, 0.0)
    mean = jnp.concatenate([mean] * PACK, axis=1)
    gain = jnp.concatenate([gain_ref[...]] * PACK, axis=1)
    shift = jnp.concatenate([shift_ref[...]] * PACK, axis=1)
    centered = hidden_ref[...].reshape(nx * ny * rows, lanes) - mean
    normalized = jnp.dot(centered, wide, precision=HIGHEST, preferred_element_type=F32)
    act = jnp.maximum(gain * normalized + shift, 0.0).reshape(hidden_ref.shape)
    clear_ends(f_ref, rows)
    f_ref[:, :, 8 : 8 + rows, :] = act
    for flag, edge in ((0, f_ref.at[0]), (1, f_ref.at[nx - 1]), (2, f_ref.at[:, 0]), (3, f_ref.at[:, ny - 1])):

        @pl.when(inside_ref[flag] == 0)
        def _(edge=edge):
            edge[...] = jnp.zeros_like(edge)

    widen(f_ref, x_ref)
    bias = jnp.concatenate([bias_ref[...]] * PACK, axis=1)
    result = banded_conv(x_ref, w_ref) + bias
    for h in range(lanes // 128):
        o_ref[h] = result[:, h * 128 : (h + 1) * 128]
    slabs, sub, _ = out_ref.shape
    for x in range(slabs):
        for b in range(rows):
            for h in range(lanes // 128):
                first = b * lanes + h * 128
                out_ref[x, :, first : first + 128] = o_ref[
                    h, pl.ds(x * sub * rows + b, sub, stride=rows), :
                ].astype(BF16)


def exchange(block, axes):
    return lax.all_to_all(block, axes, 0, 0, tiled=True)


def group_size(axes):
    return functools.reduce(lambda total, axis: total * lax.axis_size(axis), axes, 1)


def local(volume, conv_first, gain, shift, conv_second, bias_second):
    width = bias_second.shape[0]
    cx, cy, merged = volume.shape
    lanes = PACK * width
    rows = merged // lanes
    count = float(cx * group_size(GX) * cy * group_size(GY) * (merged // width))
    call = functools.partial(pl.pallas_call, compiler_params=params())
    own = call(
        rows_kernel,
        out_shape=jax.ShapeDtypeStruct((cx, cy, rows, lanes), BF16),
        scratch_shapes=[pltpu.VMEM((lanes // 128, cx * cy * rows, 128), F32)],
        name="rows",
    )(volume)
    band = call(band_kernel, out_shape=jax.ShapeDtypeStruct((lanes, 54 * width), BF16), name="band")
    first, second = band(conv_first.T), band(conv_second.T)
    xlo, xhi = shift_exchange(own[:2], own[cx - 2 :], GX)
    sides = jnp.concatenate([xlo, own, xhi], axis=0)
    ylo, yhi = shift_exchange(sides[:, :2], sides[:, cy - 2 :], GY)
    hidden, pay = call(
        hidden_kernel,
        out_shape=(
            jax.ShapeDtypeStruct((cx + 2, cy + 2, rows, lanes), F32),
            jax.ShapeDtypeStruct((group_size(GX[:1]), PAY, 1, 128), F32),
        ),
        scratch_shapes=[
            pltpu.VMEM((cx + 4, cy + 4, rows + 16, lanes), F32),
            pltpu.VMEM((cx + 4, cy + 4, rows, 6 * width), BF16),
        ],
        name="hidden",
    )(own, xlo, xhi, ylo, yhi, first)
    rest = GX[1:] + GY
    at_x, at_y = lax.axis_index(GX), lax.axis_index(GY)
    inside = jnp.stack([at_x > 0, at_x < group_size(GX) - 1, at_y > 0, at_y < group_size(GY) - 1]).astype(jnp.int32)
    pay, second, inside = lax.optimization_barrier((pay, second, inside))
    pay = exchange(pay, GX[:1])
    pay = call(
        relay_kernel, out_shape=jax.ShapeDtypeStruct((group_size(rest), PAY, 1, 128), F32), name="relay"
    )(pay)
    pay = exchange(pay, rest)
    in_vmem = pl.BlockSpec(memory_space=pltpu.VMEM)
    return call(
        functools.partial(output_kernel, count=count),
        out_shape=jax.ShapeDtypeStruct((cx, cy, merged), BF16),
        in_specs=[pl.BlockSpec(memory_space=pltpu.SMEM)] + [in_vmem] * 6,
        out_specs=in_vmem,
        scratch_shapes=[
            pltpu.VMEM((24, 128), F32),
            pltpu.VMEM((cx + 2, cy + 2, rows + 16, lanes), F32),
            pltpu.VMEM((cx + 2, cy + 2, rows, 6 * width), BF16),
            pltpu.VMEM((lanes // 128, cx * cy * rows, 128), F32),
        ],
        name="output",
    )(inside, pay, hidden, gain[None], shift[None], second, bias_second[None])


def solution(mesh):
    torus = Mesh(mesh.devices.reshape(16, 4, 4, 2), GX + GY)
    placed = (P(GX, GY, None), P(), P(), P(), P(), P())
    return jax.shard_map(
        local, mesh=torus, in_specs=placed, out_specs=P(GX, GY, None), check_vma=False
    )
```

```python
import functools

import jax
import jax.numpy as jnp
from jax import lax
from jax.experimental import pallas as pl
from jax.experimental.pallas import tpu as pltpu
from jax.sharding import Mesh
from jax.sharding import PartitionSpec as P

NEWTON = 5
GX = ("gx_0", "gx_1")
GY = ("gy_0", "gy_1")
PACK = 4
F32 = jnp.float32
BF16 = jnp.bfloat16
HIGHEST = lax.Precision.HIGHEST
PAY = 17


def params():
    return pltpu.CompilerParams(vmem_limit_bytes=48 * 1024 * 1024)


def group_size(axes):
    return functools.reduce(lambda total, axis: total * lax.axis_size(axis), axes, 1)


def swap(block, axis, first):
    pairs = [(i, i + 1) for i in range(first, lax.axis_size(axis) - 1, 2)]
    return lax.ppermute(block, axis, pairs + [(target, source) for source, target in pairs])


def to_rows(v_ref, o_ref, f_ref):
    slabs, sub, merged = v_ref.shape
    rows, lanes = o_ref.shape[2:]
    for x in range(slabs):
        for b in range(rows):
            for h in range(lanes // 128):
                first = b * lanes + h * 128
                f_ref[h, pl.ds(x * sub * rows + b, sub, stride=rows), :] = v_ref[
                    x, :, first : first + 128
                ].astype(F32)
    for h in range(lanes // 128):
        o_ref[:, :, :, h * 128 : (h + 1) * 128] = f_ref[h].astype(BF16).reshape(slabs, sub, rows, 128)


def rows_kernel(v_ref, o_ref, f_ref):
    to_rows(v_ref, o_ref, f_ref)


def edges_kernel(own_ref, xa_ref, xb_ref, xs_ref, ea_ref, eb_ref, fa_ref, fb_ref):
    cx, cy = own_ref.shape[:2]
    odd_x, odd_y = lax.axis_index(GX) & 1, lax.axis_index(GY) & 1
    to_rows(xa_ref, xs_ref.at[1 - odd_x], fa_ref)
    to_rows(xb_ref, xs_ref.at[odd_x], fb_ref)
    for edge_ref, first in ((ea_ref, (1 - odd_y) * (cy - 2)), (eb_ref, odd_y * (cy - 2))):
        edge_ref[0:2] = xs_ref[0, :, pl.ds(first, 2)]
        edge_ref[2 : 2 + cx] = own_ref[:, pl.ds(first, 2)]
        edge_ref[2 + cx : 4 + cx] = xs_ref[1, :, pl.ds(first, 2)]


def band_kernel(w_ref, o_ref):
    c = w_ref.shape[0]
    o_ref[...] = jnp.zeros_like(o_ref)
    for t in range(9):
        w = w_ref[:, t * 3 * c : (t + 1) * 3 * c]
        base = t * 6 * c
        o_ref[0:c, base : base + 2 * c] = w[:, c:]
        o_ref[0:c, base + 5 * c : base + 6 * c] = w[:, :c]
        for k in range(1, PACK):
            first = base + (k - 1) * c
            o_ref[k * c : (k + 1) * c, first : first + 3 * c] = w


def widen(f_ref, x_ref):
    rows = x_ref.shape[2]
    x_ref[:, :, :, 0:256] = f_ref[:, :, 8 : 8 + rows, :].astype(BF16)
    after = f_ref[:, :, 9 : 9 + rows, 0:128]
    before = f_ref[:, :, 7 : 7 + rows, 128:256]
    lane = lax.broadcasted_iota(jnp.int32, after.shape, 3)
    x_ref[:, :, :, 256:384] = jnp.where(lane < 64, after, before).astype(BF16)


def clear_ends(f_ref, rows):
    cells_x, cells_y, _, lanes = f_ref.shape
    zero = jnp.zeros((cells_x, cells_y, 8, lanes), F32)
    f_ref[:, :, 0:8, :] = zero
    f_ref[:, :, 8 + rows : 16 + rows, :] = zero


def banded_conv(x_ref, w_ref):
    nx, ny, rows, k = x_ref.shape
    nx, ny = nx - 2, ny - 2
    acc = None
    for dx in range(3):
        taps = [x_ref[dx : dx + nx, dy : dy + ny].reshape(nx * ny * rows, k) for dy in range(3)]
        part = lax.dot_general(
            jnp.concatenate(taps, axis=1),
            w_ref[:, dx * 3 * k : (dx + 1) * 3 * k],
            (((1,), (1,)), ((), ())),
            preferred_element_type=F32,
        )
        acc = part if acc is None else acc + part
    return acc


def square_iota(n):
    return lax.broadcasted_iota(jnp.int32, (n, n), 0), lax.broadcasted_iota(jnp.int32, (n, n), 1)


def hidden_kernel(own_ref, xs_ref, ya_ref, yb_ref, w_ref, hidden_ref, pay_ref, f_ref, x_ref):
    rows = own_ref.shape[2]
    cx, cy = own_ref.shape[:2]
    clear_ends(f_ref, rows)
    f_ref[0:2, 2 : 2 + cy, 8 : 8 + rows, :] = xs_ref[0].astype(F32)
    f_ref[2 : 2 + cx, 2 : 2 + cy, 8 : 8 + rows, :] = own_ref[...].astype(F32)
    f_ref[2 + cx : 4 + cx, 2 : 2 + cy, 8 : 8 + rows, :] = xs_ref[1].astype(F32)
    odd_y = lax.axis_index(GY) & 1
    f_ref[:, pl.ds((1 - odd_y) * (cy + 2), 2), 8 : 8 + rows, :] = ya_ref[...].astype(F32)
    f_ref[:, pl.ds(odd_y * (cy + 2), 2), 8 : 8 + rows, :] = yb_ref[...].astype(F32)
    widen(f_ref, x_ref)
    hidden_ref[...] = banded_conv(x_ref, w_ref).reshape(hidden_ref.shape)
    own = hidden_ref[1 : 1 + cx, 1 : 1 + cy].reshape(cx * cy * rows, 256)
    wide = lax.dot_general(own, own, (((0,), (0,)), ((), ())), precision=HIGHEST, preferred_element_type=F32)
    sums = jnp.sum(own, axis=0, keepdims=True)
    gram = wide[0:64, 0:64]
    total = sums[:, 0:64]
    for k in range(1, PACK):
        gram = gram + wide[k * 64 : (k + 1) * 64, k * 64 : (k + 1) * 64]
        total = total + sums[:, k * 64 : (k + 1) * 64]
    i, j = square_iota(32)
    low = gram[32:, 32:]
    tri = jnp.where(j >= i, gram[:32, :32], low)
    cross = gram[:32, 32:]
    block = jnp.concatenate([tri[:16], tri[16:], cross[:16], cross[16:]], axis=1)
    diag = jnp.sum(jnp.where(i == j, low, 0.0), axis=0, keepdims=True)
    last = jnp.concatenate([diag, total, jnp.zeros((1, 32), F32)], axis=1)
    for p in range(pay_ref.shape[0]):
        for r in range(16):
            pay_ref[p, r] = block[r : r + 1]
        pay_ref[p, 16] = last


def relay_kernel(in_ref, out_ref):
    total = jnp.sum(in_ref[...], axis=0)
    for p in range(out_ref.shape[0]):
        out_ref[p] = total


def transposed(a):
    return jnp.transpose(a)


def moments(pay_ref, p_ref, count):
    total = jnp.sum(pay_ref[...], axis=0)
    for r in range(PAY):
        p_ref[r : r + 1, :] = total[r]
    block = p_ref[0:16, :]
    last = p_ref[16:17, :]
    i, j = square_iota(32)
    tri = jnp.concatenate([block[:, 0:32], block[:, 32:64]], axis=0)
    cross = jnp.concatenate([block[:, 64:96], block[:, 96:128]], axis=0)
    flip = transposed(tri)
    top = jnp.where(j >= i, tri, flip)
    low = jnp.where(j < i, tri, flip)
    low = jnp.where(i == j, jnp.broadcast_to(last[:, 0:32], (32, 32)), low)
    gram = jnp.concatenate(
        [
            jnp.concatenate([top, cross], axis=1),
            jnp.concatenate([transposed(cross), low], axis=1),
        ],
        axis=0,
    )
    mean = last[:, 32:96] / count
    i, j = square_iota(64)
    eye = jnp.where(i == j, 1.0, 0.0).astype(F32)
    column = jnp.sum(eye * mean, axis=1, keepdims=True)
    return mean, gram / count - column * mean + 1e-05 * eye, eye


def newton_whiten(sigma, eye):
    dot = functools.partial(jnp.dot, precision=HIGHEST, preferred_element_type=F32)
    trace = jnp.sum(jnp.sum(sigma * eye, axis=1, keepdims=True), axis=0, keepdims=True)
    normed = sigma / trace
    proj = 1.5 * eye - 0.5 * normed
    for _ in range(NEWTON - 1):
        both = dot(proj, jnp.concatenate([proj, normed], axis=1))
        proj = 1.5 * proj - 0.5 * dot(both[:, 0:64], both[:, 64:128])
    return proj / jnp.sqrt(trace)


def output_kernel(
    pay_ref, hidden_ref, gain_ref, shift_ref, w_ref, bias_ref, out_ref, p_ref, f_ref, x_ref, o_ref, *, count
):
    nx, ny, rows, lanes = hidden_ref.shape
    mean, sigma, eye = moments(pay_ref, p_ref, count)
    whiten = newton_whiten(sigma, eye)
    i, j = square_iota(lanes)
    wide = jnp.concatenate([whiten] * PACK, axis=1)
    wide = jnp.concatenate([wide] * PACK, axis=0)
    wide = jnp.where(i >> 6 == j >> 6, wide, 0.0)
    mean = jnp.concatenate([mean] * PACK, axis=1)
    gain = jnp.concatenate([gain_ref[...]] * PACK, axis=1)
    shift = jnp.concatenate([shift_ref[...]] * PACK, axis=1)
    centered = hidden_ref[...].reshape(nx * ny * rows, lanes) - mean
    normalized = jnp.dot(centered, wide, precision=HIGHEST, preferred_element_type=F32)
    act = jnp.maximum(gain * normalized + shift, 0.0).reshape(hidden_ref.shape)
    clear_ends(f_ref, rows)
    f_ref[:, :, 8 : 8 + rows, :] = act
    at_x, at_y = lax.axis_index(GX), lax.axis_index(GY)
    for outside, edge in (
        (at_x == 0, f_ref.at[0]),
        (at_x == group_size(GX) - 1, f_ref.at[nx - 1]),
        (at_y == 0, f_ref.at[:, 0]),
        (at_y == group_size(GY) - 1, f_ref.at[:, ny - 1]),
    ):

        @pl.when(outside)
        def _(edge=edge):
            edge[...] = jnp.zeros_like(edge)

    widen(f_ref, x_ref)
    bias = jnp.concatenate([bias_ref[...]] * PACK, axis=1)
    result = banded_conv(x_ref, w_ref) + bias
    for h in range(lanes // 128):
        o_ref[h] = result[:, h * 128 : (h + 1) * 128]
    slabs, sub, _ = out_ref.shape
    for x in range(slabs):
        for b in range(rows):
            for h in range(lanes // 128):
                first = b * lanes + h * 128
                out_ref[x, :, first : first + 128] = o_ref[
                    h, pl.ds(x * sub * rows + b, sub, stride=rows), :
                ].astype(BF16)


def exchange(block, axes):
    return lax.all_to_all(block, axes, 0, 0, tiled=True)


def local(volume, conv_first, gain, shift, conv_second, bias_second):
    width = bias_second.shape[0]
    cx, cy, merged = volume.shape
    lanes = PACK * width
    rows = merged // lanes
    count = float(cx * group_size(GX) * cy * group_size(GY) * (merged // width))
    call = functools.partial(pl.pallas_call, compiler_params=params())
    xa, xb = swap(volume, GX, 0), swap(volume, GX, 1)
    block = jax.ShapeDtypeStruct((cx, cy, rows, lanes), BF16)
    half = pltpu.VMEM((lanes // 128, cx * cy * rows, 128), F32)
    own = call(rows_kernel, out_shape=block, scratch_shapes=[half], name="rows")(volume)
    band = call(band_kernel, out_shape=jax.ShapeDtypeStruct((lanes, 54 * width), BF16), name="band")
    first, second = band(conv_first.T), band(conv_second.T)
    edge = jax.ShapeDtypeStruct((cx + 4, 2, rows, lanes), BF16)
    xs, ea, eb = call(
        edges_kernel,
        out_shape=(jax.ShapeDtypeStruct((2,) + block.shape, BF16), edge, edge),
        scratch_shapes=[half, half],
        name="edges",
    )(own, xa, xb)
    ya, yb = swap(ea, GY, 0), swap(eb, GY, 1)
    hidden, pay = call(
        hidden_kernel,
        out_shape=(
            jax.ShapeDtypeStruct((cx + 2, cy + 2, rows, lanes), F32),
            jax.ShapeDtypeStruct((group_size(GX[:1]), PAY, 1, 128), F32),
        ),
        scratch_shapes=[
            pltpu.VMEM((cx + 4, cy + 4, rows + 16, lanes), F32),
            pltpu.VMEM((cx + 4, cy + 4, rows, 6 * width), BF16),
        ],
        name="hidden",
    )(own, xs, ya, yb, first)
    rest = GX[1:] + GY
    pay, second = lax.optimization_barrier((pay, second))
    pay = exchange(pay, GX[:1])
    pay = call(
        relay_kernel, out_shape=jax.ShapeDtypeStruct((group_size(rest), PAY, 1, 128), F32), name="relay"
    )(pay)
    pay = exchange(pay, rest)
    return call(
        functools.partial(output_kernel, count=count),
        out_shape=jax.ShapeDtypeStruct((cx, cy, merged), BF16),
        scratch_shapes=[
            pltpu.VMEM((24, 128), F32),
            pltpu.VMEM((cx + 2, cy + 2, rows + 16, lanes), F32),
            pltpu.VMEM((cx + 2, cy + 2, rows, 6 * width), BF16),
            pltpu.VMEM((lanes // 128, cx * cy * rows, 128), F32),
        ],
        name="output",
    )(pay, hidden, gain[None], shift[None], second, bias_second[None])


def solution(mesh):
    torus = Mesh(mesh.devices.reshape(16, 4, 4, 2), GX + GY)
    placed = (P(GX, GY, None), P(), P(), P(), P(), P())
    return jax.shard_map(
        local, mesh=torus, in_specs=placed, out_specs=P(GX, GY, None), check_vma=False
    )
```

```python
import functools

import jax
import jax.numpy as jnp
from jax import lax
from jax.experimental import pallas as pl
from jax.experimental.pallas import tpu as pltpu
from jax.sharding import Mesh
from jax.sharding import PartitionSpec as P

NEWTON = 5
GX = ("gx_0", "gx_1")
GY = ("gy_0", "gy_1")
PACK = 4
F32 = jnp.float32
BF16 = jnp.bfloat16
HIGHEST = lax.Precision.HIGHEST
PAY = 17


def params():
    return pltpu.CompilerParams(vmem_limit_bytes=48 * 1024 * 1024)


def group_size(axes):
    return functools.reduce(lambda total, axis: total * lax.axis_size(axis), axes, 1)


def swap(block, axis, first):
    pairs = [(i, i + 1) for i in range(first, lax.axis_size(axis) - 1, 2)]
    return lax.ppermute(block, axis, pairs + [(target, source) for source, target in pairs])


def to_rows(v_ref, o_ref, f_ref):
    slabs, sub, merged = v_ref.shape
    rows, lanes = o_ref.shape[2:]
    for x in range(slabs):
        for b in range(rows):
            for h in range(lanes // 128):
                first = b * lanes + h * 128
                f_ref[h, pl.ds(x * sub * rows + b, sub, stride=rows), :] = v_ref[
                    x, :, first : first + 128
                ].astype(F32)
    for h in range(lanes // 128):
        o_ref[:, :, :, h * 128 : (h + 1) * 128] = f_ref[h].astype(BF16).reshape(slabs, sub, rows, 128)


def rows_kernel(v_ref, o_ref, f_ref):
    to_rows(v_ref, o_ref, f_ref)


def edges_kernel(own_ref, xa_ref, xb_ref, xs_ref, ea_ref, eb_ref, fa_ref, fb_ref):
    cx, cy = own_ref.shape[:2]
    odd_x, odd_y = lax.axis_index(GX) & 1, lax.axis_index(GY) & 1
    to_rows(xa_ref, xs_ref.at[1 - odd_x], fa_ref)
    to_rows(xb_ref, xs_ref.at[odd_x], fb_ref)
    for edge_ref, first in ((ea_ref, (1 - odd_y) * (cy - 2)), (eb_ref, odd_y * (cy - 2))):
        edge_ref[0:2] = xs_ref[0, :, pl.ds(first, 2)]
        edge_ref[2 : 2 + cx] = own_ref[:, pl.ds(first, 2)]
        edge_ref[2 + cx : 4 + cx] = xs_ref[1, :, pl.ds(first, 2)]


def band_kernel(w_ref, o_ref):
    c = w_ref.shape[0]
    o_ref[...] = jnp.zeros_like(o_ref)
    for t in range(9):
        w = w_ref[:, t * 3 * c : (t + 1) * 3 * c]
        base = t * 6 * c
        o_ref[0:c, base : base + 2 * c] = w[:, c:]
        o_ref[0:c, base + 5 * c : base + 6 * c] = w[:, :c]
        for k in range(1, PACK):
            first = base + (k - 1) * c
            o_ref[k * c : (k + 1) * c, first : first + 3 * c] = w


def widen(f_ref, x_ref):
    rows = x_ref.shape[2]
    x_ref[:, :, :, 0:256] = f_ref[:, :, 8 : 8 + rows, :].astype(BF16)
    after = f_ref[:, :, 9 : 9 + rows, 0:128]
    before = f_ref[:, :, 7 : 7 + rows, 128:256]
    lane = lax.broadcasted_iota(jnp.int32, after.shape, 3)
    x_ref[:, :, :, 256:384] = jnp.where(lane < 64, after, before).astype(BF16)


def clear_ends(f_ref, rows):
    cells_x, cells_y, _, lanes = f_ref.shape
    zero = jnp.zeros((cells_x, cells_y, 8, lanes), F32)
    f_ref[:, :, 0:8, :] = zero
    f_ref[:, :, 8 + rows : 16 + rows, :] = zero


def banded_conv(x_ref, w_ref):
    nx, ny, rows, k = x_ref.shape
    nx, ny = nx - 2, ny - 2
    acc = None
    for dx in range(3):
        taps = [x_ref[dx : dx + nx, dy : dy + ny].reshape(nx * ny * rows, k) for dy in range(3)]
        part = lax.dot_general(
            jnp.concatenate(taps, axis=1),
            w_ref[:, dx * 3 * k : (dx + 1) * 3 * k],
            (((1,), (1,)), ((), ())),
            preferred_element_type=F32,
        )
        acc = part if acc is None else acc + part
    return acc


def square_iota(n):
    return lax.broadcasted_iota(jnp.int32, (n, n), 0), lax.broadcasted_iota(jnp.int32, (n, n), 1)


def transposed(a):
    return jnp.transpose(a)


def split(a):
    high = a.astype(BF16)
    return high, (a - high.astype(F32)).astype(BF16)


def dot3(a, b):
    dot = functools.partial(jnp.dot, preferred_element_type=F32)
    a0, a1 = split(a)
    b0, b1 = split(b)
    return dot(a0, b0) + (dot(a0, b1) + dot(a1, b0))


def fold_blocks(wide):
    total = wide[0:64, 0:64]
    for k in range(1, PACK):
        total = total + wide[k * 64 : (k + 1) * 64, k * 64 : (k + 1) * 64]
    return total


def hidden_kernel(own_ref, xs_ref, yb_ref, ya_ref, w_ref, hidden_ref, pay_ref, f_ref, x_ref):
    rows = own_ref.shape[2]
    cx, cy = own_ref.shape[:2]
    clear_ends(f_ref, rows)
    f_ref[0:2, 2 : 2 + cy, 8 : 8 + rows, :] = xs_ref[0].astype(F32)
    f_ref[2 : 2 + cx, 2 : 2 + cy, 8 : 8 + rows, :] = own_ref[...].astype(F32)
    f_ref[2 + cx : 4 + cx, 2 : 2 + cy, 8 : 8 + rows, :] = xs_ref[1].astype(F32)
    odd_y = lax.axis_index(GY) & 1
    f_ref[:, pl.ds((1 - odd_y) * (cy + 2), 2), 8 : 8 + rows, :] = ya_ref[...].astype(F32)
    f_ref[:, pl.ds(odd_y * (cy + 2), 2), 8 : 8 + rows, :] = yb_ref[...].astype(F32)
    widen(f_ref, x_ref)
    hidden_ref[...] = banded_conv(x_ref, w_ref).reshape(hidden_ref.shape)
    own = hidden_ref[1 : 1 + cx, 1 : 1 + cy].reshape(cx * cy * rows, 256)
    sums = jnp.sum(own, axis=0, keepdims=True)
    total = sums[:, 0:64]
    for k in range(1, PACK):
        total = total + sums[:, k * 64 : (k + 1) * 64]
    cells = float(cx * cy * rows * PACK)
    high, low = split(own - jnp.concatenate([total / cells] * PACK, axis=1))
    outer = functools.partial(
        lax.dot_general, dimension_numbers=(((0,), (0,)), ((), ())), preferred_element_type=F32
    )
    mixed = fold_blocks(outer(high, low))
    i, j = square_iota(64)
    column = jnp.sum(jnp.where(i == j, total, 0.0), axis=1, keepdims=True)
    gram = fold_blocks(outer(high, high)) + (mixed + transposed(mixed)) + column * (total / cells)
    i, j = square_iota(32)
    low = gram[32:, 32:]
    tri = jnp.where(j >= i, gram[:32, :32], low)
    cross = gram[:32, 32:]
    block = jnp.concatenate([tri[:16], tri[16:], cross[:16], cross[16:]], axis=1)
    diag = jnp.sum(jnp.where(i == j, low, 0.0), axis=0, keepdims=True)
    last = jnp.concatenate([diag, total, jnp.zeros((1, 32), F32)], axis=1)
    for p in range(pay_ref.shape[0]):
        for r in range(16):
            pay_ref[p, r] = block[r : r + 1]
        pay_ref[p, 16] = last


def relay_kernel(in_ref, out_ref):
    total = jnp.sum(in_ref[...], axis=0)
    for p in range(out_ref.shape[0]):
        out_ref[p] = total


def moments(pay_ref, p_ref, count):
    total = jnp.sum(pay_ref[...], axis=0)
    for r in range(PAY):
        p_ref[r : r + 1, :] = total[r]
    block = p_ref[0:16, :]
    last = p_ref[16:17, :]
    i, j = square_iota(32)
    tri = jnp.concatenate([block[:, 0:32], block[:, 32:64]], axis=0)
    cross = jnp.concatenate([block[:, 64:96], block[:, 96:128]], axis=0)
    flip = transposed(tri)
    top = jnp.where(j >= i, tri, flip)
    low = jnp.where(j < i, tri, flip)
    low = jnp.where(i == j, jnp.broadcast_to(last[:, 0:32], (32, 32)), low)
    gram = jnp.concatenate(
        [
            jnp.concatenate([top, cross], axis=1),
            jnp.concatenate([transposed(cross), low], axis=1),
        ],
        axis=0,
    )
    mean = last[:, 32:96] / count
    i, j = square_iota(64)
    eye = jnp.where(i == j, 1.0, 0.0).astype(F32)
    column = jnp.sum(eye * mean, axis=1, keepdims=True)
    return mean, gram / count - column * mean + 1e-05 * eye, eye


def newton_whiten(sigma, eye):
    trace = jnp.sum(jnp.sum(sigma * eye, axis=1, keepdims=True), axis=0, keepdims=True)
    normed = sigma / trace
    proj = 1.5 * eye - 0.5 * normed
    for _ in range(NEWTON - 1):
        both = dot3(proj, jnp.concatenate([proj, normed], axis=1))
        proj = 1.5 * proj - 0.5 * dot3(both[:, 0:64], both[:, 64:128])
    return proj / jnp.sqrt(trace)


def output_kernel(
    pay_ref, hidden_ref, gain_ref, shift_ref, w_ref, bias_ref, out_ref, p_ref, f_ref, x_ref, o_ref, *, count
):
    nx, ny, rows, lanes = hidden_ref.shape
    mean, sigma, eye = moments(pay_ref, p_ref, count)
    whiten = newton_whiten(sigma, eye)
    i, j = square_iota(lanes)
    wide = jnp.concatenate([whiten] * PACK, axis=1)
    wide = jnp.concatenate([wide] * PACK, axis=0)
    wide = jnp.where(i >> 6 == j >> 6, wide, 0.0)
    mean = jnp.concatenate([mean] * PACK, axis=1)
    gain = jnp.concatenate([gain_ref[...]] * PACK, axis=1)
    shift = jnp.concatenate([shift_ref[...]] * PACK, axis=1)
    centered = hidden_ref[...].reshape(nx * ny * rows, lanes) - mean
    normalized = dot3(centered, wide)
    act = jnp.maximum(gain * normalized + shift, 0.0).reshape(hidden_ref.shape)
    clear_ends(f_ref, rows)
    f_ref[:, :, 8 : 8 + rows, :] = act
    at_x, at_y = lax.axis_index(GX), lax.axis_index(GY)
    for outside, edge in (
        (at_x == 0, f_ref.at[0]),
        (at_x == group_size(GX) - 1, f_ref.at[nx - 1]),
        (at_y == 0, f_ref.at[:, 0]),
        (at_y == group_size(GY) - 1, f_ref.at[:, ny - 1]),
    ):

        @pl.when(outside)
        def _(edge=edge):
            edge[...] = jnp.zeros_like(edge)

    widen(f_ref, x_ref)
    bias = jnp.concatenate([bias_ref[...]] * PACK, axis=1)
    result = banded_conv(x_ref, w_ref) + bias
    for h in range(lanes // 128):
        o_ref[h] = result[:, h * 128 : (h + 1) * 128]
    slabs, sub, _ = out_ref.shape
    for x in range(slabs):
        for b in range(rows):
            for h in range(lanes // 128):
                first = b * lanes + h * 128
                out_ref[x, :, first : first + 128] = o_ref[
                    h, pl.ds(x * sub * rows + b, sub, stride=rows), :
                ].astype(BF16)


def exchange(block, axes):
    return lax.all_to_all(block, axes, 0, 0, tiled=True)


def local(volume, conv_first, gain, shift, conv_second, bias_second):
    width = bias_second.shape[0]
    cx, cy, merged = volume.shape
    lanes = PACK * width
    rows = merged // lanes
    count = float(cx * group_size(GX) * cy * group_size(GY) * (merged // width))
    call = functools.partial(pl.pallas_call, compiler_params=params())
    xa, xb = swap(volume, GX, 0), swap(volume, GX, 1)
    block = jax.ShapeDtypeStruct((cx, cy, rows, lanes), BF16)
    half = pltpu.VMEM((lanes // 128, cx * cy * rows, 128), F32)
    own = call(rows_kernel, out_shape=block, scratch_shapes=[half], name="rows")(volume)
    band = call(band_kernel, out_shape=jax.ShapeDtypeStruct((lanes, 54 * width), BF16), name="band")
    first, second = band(conv_first.T), band(conv_second.T)
    xb, first, second = lax.optimization_barrier((xb, first, second))
    edge = jax.ShapeDtypeStruct((cx + 4, 2, rows, lanes), BF16)
    xs, ea, eb = call(
        edges_kernel,
        out_shape=(jax.ShapeDtypeStruct((2,) + block.shape, BF16), edge, edge),
        scratch_shapes=[half, half],
        name="edges",
    )(own, xa, xb)
    yb = swap(eb, GY, 1)
    ya = swap(ea, GY, 0)
    hidden, pay = call(
        hidden_kernel,
        out_shape=(
            jax.ShapeDtypeStruct((cx + 2, cy + 2, rows, lanes), F32),
            jax.ShapeDtypeStruct((group_size(GX[1:] + GY), PAY, 1, 128), F32),
        ),
        scratch_shapes=[
            pltpu.VMEM((cx + 4, cy + 4, rows + 16, lanes), F32),
            pltpu.VMEM((cx + 4, cy + 4, rows, 6 * width), BF16),
        ],
        name="hidden",
    )(own, xs, yb, ya, first)
    rest, line = GX[1:] + GY, GX[:1]
    pay = exchange(pay, rest)
    pay = call(
        relay_kernel, out_shape=jax.ShapeDtypeStruct((group_size(line), PAY, 1, 128), F32), name="relay"
    )(pay)
    pay = exchange(pay, line)
    return call(
        functools.partial(output_kernel, count=count),
        out_shape=jax.ShapeDtypeStruct((cx, cy, merged), BF16),
        scratch_shapes=[
            pltpu.VMEM((24, 128), F32),
            pltpu.VMEM((cx + 2, cy + 2, rows + 16, lanes), F32),
            pltpu.VMEM((cx + 2, cy + 2, rows, 6 * width), BF16),
            pltpu.VMEM((lanes // 128, cx * cy * rows, 128), F32),
        ],
        name="output",
    )(pay, hidden, gain[None], shift[None], second, bias_second[None])


def solution(mesh):
    torus = Mesh(mesh.devices.reshape(16, 4, 4, 2), GX + GY)
    placed = (P(GX, GY, None), P(), P(), P(), P(), P())
    return jax.shard_map(
        local, mesh=torus, in_specs=placed, out_specs=P(GX, GY, None), check_vma=False
    )
```

```python
import functools

import jax
import jax.numpy as jnp
from jax import lax
from jax.experimental import pallas as pl
from jax.experimental.pallas import tpu as pltpu
from jax.sharding import Mesh
from jax.sharding import PartitionSpec as P

NEWTON = 5
GX = ("gx_0", "gx_1")
GY = ("gy_0", "gy_1")
PACK = 4
F32 = jnp.float32
BF16 = jnp.bfloat16
HIGHEST = lax.Precision.HIGHEST
PAY = 24


def params():
    return pltpu.CompilerParams(vmem_limit_bytes=48 * 1024 * 1024)


def group_size(axes):
    return functools.reduce(lambda total, axis: total * lax.axis_size(axis), axes, 1)


def swap(block, axis, first):
    pairs = [(i, i + 1) for i in range(first, lax.axis_size(axis) - 1, 2)]
    return lax.ppermute(block, axis, pairs + [(target, source) for source, target in pairs])


def to_rows(v_ref, o_ref, f_ref):
    slabs, sub, merged = v_ref.shape
    rows, lanes = o_ref.shape[2:]
    for x in range(slabs):
        for b in range(rows):
            for h in range(lanes // 128):
                first = b * lanes + h * 128
                f_ref[h, pl.ds(x * sub * rows + b, sub, stride=rows), :] = v_ref[
                    x, :, first : first + 128
                ].astype(F32)
    for h in range(lanes // 128):
        o_ref[:, :, :, h * 128 : (h + 1) * 128] = f_ref[h].astype(BF16).reshape(slabs, sub, rows, 128)


def rows_kernel(v_ref, o_ref, f_ref):
    to_rows(v_ref, o_ref, f_ref)


def edges_kernel(own_ref, xa_ref, xb_ref, xs_ref, ea_ref, eb_ref, fa_ref, fb_ref):
    cx, cy = own_ref.shape[:2]
    odd_x, odd_y = lax.axis_index(GX) & 1, lax.axis_index(GY) & 1
    to_rows(xa_ref, xs_ref.at[1 - odd_x], fa_ref)
    to_rows(xb_ref, xs_ref.at[odd_x], fb_ref)
    for edge_ref, first in ((ea_ref, (1 - odd_y) * (cy - 2)), (eb_ref, odd_y * (cy - 2))):
        edge_ref[0:2] = xs_ref[0, :, pl.ds(first, 2)]
        edge_ref[2 : 2 + cx] = own_ref[:, pl.ds(first, 2)]
        edge_ref[2 + cx : 4 + cx] = xs_ref[1, :, pl.ds(first, 2)]


def band_kernel(w_ref, o_ref):
    c = w_ref.shape[0]
    o_ref[...] = jnp.zeros_like(o_ref)
    for t in range(9):
        w = w_ref[:, t * 3 * c : (t + 1) * 3 * c]
        base = t * 6 * c
        o_ref[0:c, base : base + 2 * c] = w[:, c:]
        o_ref[0:c, base + 5 * c : base + 6 * c] = w[:, :c]
        for k in range(1, PACK):
            first = base + (k - 1) * c
            o_ref[k * c : (k + 1) * c, first : first + 3 * c] = w


def widen(f_ref, x_ref):
    rows = x_ref.shape[2]
    x_ref[:, :, :, 0:256] = f_ref[:, :, 8 : 8 + rows, :].astype(BF16)
    after = f_ref[:, :, 9 : 9 + rows, 0:128]
    before = f_ref[:, :, 7 : 7 + rows, 128:256]
    lane = lax.broadcasted_iota(jnp.int32, after.shape, 3)
    x_ref[:, :, :, 256:384] = jnp.where(lane < 64, after, before).astype(BF16)


def clear_ends(f_ref, rows):
    cells_x, cells_y, _, lanes = f_ref.shape
    zero = jnp.zeros((cells_x, cells_y, 8, lanes), F32)
    f_ref[:, :, 0:8, :] = zero
    f_ref[:, :, 8 + rows : 16 + rows, :] = zero


def banded_conv(x_ref, w_ref):
    nx, ny, rows, k = x_ref.shape
    nx, ny = nx - 2, ny - 2
    acc = None
    for dx in range(3):
        taps = [x_ref[dx : dx + nx, dy : dy + ny].reshape(nx * ny * rows, k) for dy in range(3)]
        part = lax.dot_general(
            jnp.concatenate(taps, axis=1),
            w_ref[:, dx * 3 * k : (dx + 1) * 3 * k],
            (((1,), (1,)), ((), ())),
            preferred_element_type=F32,
        )
        acc = part if acc is None else acc + part
    return acc


def square_iota(n):
    return lax.broadcasted_iota(jnp.int32, (n, n), 0), lax.broadcasted_iota(jnp.int32, (n, n), 1)


def transposed(a):
    return jnp.transpose(a)


def split(a):
    high = a.astype(BF16)
    return high, (a - high.astype(F32)).astype(BF16)


def dot3(a, b):
    dot = functools.partial(jnp.dot, preferred_element_type=F32)
    a0, a1 = split(a)
    b0, b1 = split(b)
    return dot(a0, b0) + (dot(a0, b1) + dot(a1, b0))


def fold_blocks(wide):
    total = wide[0:64, 0:64]
    for k in range(1, PACK):
        total = total + wide[k * 64 : (k + 1) * 64, k * 64 : (k + 1) * 64]
    return total


def hidden_kernel(own_ref, xs_ref, yb_ref, ya_ref, w_ref, hidden_ref, pay_ref, f_ref, x_ref, p_ref):
    rows = own_ref.shape[2]
    cx, cy = own_ref.shape[:2]
    clear_ends(f_ref, rows)
    f_ref[0:2, 2 : 2 + cy, 8 : 8 + rows, :] = xs_ref[0].astype(F32)
    f_ref[2 : 2 + cx, 2 : 2 + cy, 8 : 8 + rows, :] = own_ref[...].astype(F32)
    f_ref[2 + cx : 4 + cx, 2 : 2 + cy, 8 : 8 + rows, :] = xs_ref[1].astype(F32)
    odd_y = lax.axis_index(GY) & 1
    f_ref[:, pl.ds((1 - odd_y) * (cy + 2), 2), 8 : 8 + rows, :] = ya_ref[...].astype(F32)
    f_ref[:, pl.ds(odd_y * (cy + 2), 2), 8 : 8 + rows, :] = yb_ref[...].astype(F32)
    widen(f_ref, x_ref)
    hidden_ref[...] = banded_conv(x_ref, w_ref).reshape(hidden_ref.shape)
    own = hidden_ref[1 : 1 + cx, 1 : 1 + cy].reshape(cx * cy * rows, 256)
    sums = jnp.sum(own, axis=0, keepdims=True)
    total = sums[:, 0:64]
    for k in range(1, PACK):
        total = total + sums[:, k * 64 : (k + 1) * 64]
    cells = float(cx * cy * rows * PACK)
    high, low = split(own - jnp.concatenate([total / cells] * PACK, axis=1))
    outer = functools.partial(
        lax.dot_general, dimension_numbers=(((0,), (0,)), ((), ())), preferred_element_type=F32
    )
    mixed = fold_blocks(outer(high, low))
    gram = fold_blocks(outer(high, high)) + (mixed + transposed(mixed))
    pack(gram, total, pay_ref, p_ref)


def pack(cov, total, pay_ref, p_ref):
    i, j = square_iota(32)
    low = cov[32:, 32:]
    tri = jnp.where(j >= i, cov[:32, :32], low)
    cross = cov[:32, 32:]
    p_ref[0:16, :] = jnp.concatenate([tri[:16], tri[16:], cross[:16], cross[16:]], axis=1)
    p_ref[16:24, :] = jnp.zeros((8, 128), F32)
    p_ref[16:17, 0:32] = jnp.sum(jnp.where(i == j, low, 0.0), axis=0, keepdims=True)
    for r in range(16, 19):
        part = total.astype(BF16).astype(F32)
        p_ref[r : r + 1, 32:96] = part
        total = total - part
    block = p_ref[...].astype(BF16)
    for p in range(pay_ref.shape[0]):
        pay_ref[p] = block


def combine(pay_ref, p_ref, cells):
    each = pay_ref[...].astype(F32)
    p_ref[...] = jnp.sum(each, axis=0)
    block = p_ref[0:16, :]
    diag = p_ref[16:17, 0:32]
    sums = jnp.sum(each[:, 16:24, :], axis=1)[:, 32:96]
    total = jnp.sum(sums, axis=0, keepdims=True)
    apart = sums / cells - total / (cells * pay_ref.shape[0])
    between = lax.dot_general(
        apart, apart * cells, (((0,), (0,)), ((), ())), precision=HIGHEST, preferred_element_type=F32
    )
    i, j = square_iota(32)
    tri = jnp.concatenate([block[:, 0:32], block[:, 32:64]], axis=0)
    cross = jnp.concatenate([block[:, 64:96], block[:, 96:128]], axis=0)
    flip = transposed(tri)
    top = jnp.where(j >= i, tri, flip)
    low = jnp.where(j < i, tri, flip)
    low = jnp.where(i == j, jnp.broadcast_to(diag, (32, 32)), low)
    upper = jnp.concatenate([top, cross], axis=1)
    lower = jnp.concatenate([transposed(cross), low], axis=1)
    return jnp.concatenate([upper, lower], axis=0) + between, total


def relay_kernel(in_ref, out_ref, p_ref, *, cells):
    cov, total = combine(in_ref, p_ref, cells)
    pack(cov, total, out_ref, p_ref)


def newton_whiten(sigma, eye):
    trace = jnp.sum(jnp.sum(sigma * eye, axis=1, keepdims=True), axis=0, keepdims=True)
    normed = sigma / trace
    proj = 1.5 * eye - 0.5 * normed
    for _ in range(NEWTON - 1):
        both = dot3(proj, jnp.concatenate([proj, normed], axis=1))
        proj = 1.5 * proj - 0.5 * dot3(both[:, 0:64], both[:, 64:128])
    return proj / jnp.sqrt(trace)


def output_kernel(
    pay_ref, hidden_ref, gain_ref, shift_ref, w_ref, bias_ref, out_ref, p_ref, f_ref, x_ref, o_ref, *, count
):
    nx, ny, rows, lanes = hidden_ref.shape
    cov, total = combine(pay_ref, p_ref, count / pay_ref.shape[0])
    i, j = square_iota(64)
    eye = jnp.where(i == j, 1.0, 0.0).astype(F32)
    mean = total / count
    sigma = cov / count + 1e-05 * eye
    whiten = newton_whiten(sigma, eye)
    i, j = square_iota(lanes)
    wide = jnp.concatenate([whiten] * PACK, axis=1)
    wide = jnp.concatenate([wide] * PACK, axis=0)
    wide = jnp.where(i >> 6 == j >> 6, wide, 0.0)
    mean = jnp.concatenate([mean] * PACK, axis=1)
    gain = jnp.concatenate([gain_ref[...]] * PACK, axis=1)
    shift = jnp.concatenate([shift_ref[...]] * PACK, axis=1)
    centered = hidden_ref[...].reshape(nx * ny * rows, lanes) - mean
    normalized = dot3(centered, wide)
    act = jnp.maximum(gain * normalized + shift, 0.0).reshape(hidden_ref.shape)
    clear_ends(f_ref, rows)
    f_ref[:, :, 8 : 8 + rows, :] = act
    at_x, at_y = lax.axis_index(GX), lax.axis_index(GY)
    for outside, edge in (
        (at_x == 0, f_ref.at[0]),
        (at_x == group_size(GX) - 1, f_ref.at[nx - 1]),
        (at_y == 0, f_ref.at[:, 0]),
        (at_y == group_size(GY) - 1, f_ref.at[:, ny - 1]),
    ):

        @pl.when(outside)
        def _(edge=edge):
            edge[...] = jnp.zeros_like(edge)

    widen(f_ref, x_ref)
    bias = jnp.concatenate([bias_ref[...]] * PACK, axis=1)
    result = banded_conv(x_ref, w_ref) + bias
    for h in range(lanes // 128):
        o_ref[h] = result[:, h * 128 : (h + 1) * 128]
    slabs, sub, _ = out_ref.shape
    for x in range(slabs):
        for b in range(rows):
            for h in range(lanes // 128):
                first = b * lanes + h * 128
                out_ref[x, :, first : first + 128] = o_ref[
                    h, pl.ds(x * sub * rows + b, sub, stride=rows), :
                ].astype(BF16)


def exchange(block, axes):
    return lax.all_to_all(block, axes, 0, 0, tiled=True)


def local(volume, conv_first, gain, shift, conv_second, bias_second):
    width = bias_second.shape[0]
    cx, cy, merged = volume.shape
    lanes = PACK * width
    rows = merged // lanes
    count = float(cx * group_size(GX) * cy * group_size(GY) * (merged // width))
    rest, line = GX[1:] + GY, GX[:1]
    packed = pltpu.VMEM((PAY, 128), F32)
    call = functools.partial(pl.pallas_call, compiler_params=params())
    xa, xb = swap(volume, GX, 0), swap(volume, GX, 1)
    block = jax.ShapeDtypeStruct((cx, cy, rows, lanes), BF16)
    half = pltpu.VMEM((lanes // 128, cx * cy * rows, 128), F32)
    own = call(rows_kernel, out_shape=block, scratch_shapes=[half], name="rows")(volume)
    band = call(band_kernel, out_shape=jax.ShapeDtypeStruct((lanes, 54 * width), BF16), name="band")
    first, second = band(conv_first.T), band(conv_second.T)
    xb, first, second = lax.optimization_barrier((xb, first, second))
    edge = jax.ShapeDtypeStruct((cx + 4, 2, rows, lanes), BF16)
    xs, ea, eb = call(
        edges_kernel,
        out_shape=(jax.ShapeDtypeStruct((2,) + block.shape, BF16), edge, edge),
        scratch_shapes=[half, half],
        name="edges",
    )(own, xa, xb)
    yb = swap(eb, GY, 1)
    ya = swap(ea, GY, 0)
    hidden, pay = call(
        hidden_kernel,
        out_shape=(
            jax.ShapeDtypeStruct((cx + 2, cy + 2, rows, lanes), F32),
            jax.ShapeDtypeStruct((group_size(rest), PAY, 128), BF16),
        ),
        scratch_shapes=[
            pltpu.VMEM((cx + 4, cy + 4, rows + 16, lanes), F32),
            pltpu.VMEM((cx + 4, cy + 4, rows, 6 * width), BF16),
            packed,
        ],
        name="hidden",
    )(own, xs, yb, ya, first)
    pay = exchange(pay, rest)
    pay = call(
        functools.partial(relay_kernel, cells=float(cx * cy * (merged // width))),
        out_shape=jax.ShapeDtypeStruct((group_size(line), PAY, 128), BF16),
        scratch_shapes=[packed],
        name="relay",
    )(pay)
    pay = exchange(pay, line)
    return call(
        functools.partial(output_kernel, count=count),
        out_shape=jax.ShapeDtypeStruct((cx, cy, merged), BF16),
        scratch_shapes=[
            packed,
            pltpu.VMEM((cx + 2, cy + 2, rows + 16, lanes), F32),
            pltpu.VMEM((cx + 2, cy + 2, rows, 6 * width), BF16),
            pltpu.VMEM((lanes // 128, cx * cy * rows, 128), F32),
        ],
        name="output",
    )(pay, hidden, gain[None], shift[None], second, bias_second[None])


def solution(mesh):
    torus = Mesh(mesh.devices.reshape(16, 4, 4, 2), GX + GY)
    placed = (P(GX, GY, None), P(), P(), P(), P(), P())
    return jax.shard_map(
        local, mesh=torus, in_specs=placed, out_specs=P(GX, GY, None), check_vma=False
    )
```

```python
import functools

import jax
import jax.numpy as jnp
from jax import lax
from jax.experimental import pallas as pl
from jax.experimental.pallas import tpu as pltpu
from jax.sharding import Mesh
from jax.sharding import PartitionSpec as P

NEWTON = 5
GX = ("gx_0", "gx_1")
GY = ("gy_0", "gy_1")
PACK = 4
F32 = jnp.float32
BF16 = jnp.bfloat16
HIGHEST = lax.Precision.HIGHEST
PAY = 17


def params():
    return pltpu.CompilerParams(vmem_limit_bytes=48 * 1024 * 1024)


def group_size(axes):
    return functools.reduce(lambda total, axis: total * lax.axis_size(axis), axes, 1)


def swap(block, axis, first):
    pairs = [(i, i + 1) for i in range(first, lax.axis_size(axis) - 1, 2)]
    return lax.ppermute(block, axis, pairs + [(target, source) for source, target in pairs])


def to_rows(v_ref, o_ref, f_ref):
    slabs, sub, merged = v_ref.shape
    rows, lanes = o_ref.shape[2:]
    for x in range(slabs):
        for b in range(rows):
            for h in range(lanes // 128):
                first = b * lanes + h * 128
                f_ref[h, pl.ds(x * sub * rows + b, sub, stride=rows), :] = v_ref[
                    x, :, first : first + 128
                ].astype(F32)
    for h in range(lanes // 128):
        o_ref[:, :, :, h * 128 : (h + 1) * 128] = f_ref[h].astype(BF16).reshape(slabs, sub, rows, 128)


def rows_kernel(v_ref, o_ref, f_ref):
    to_rows(v_ref, o_ref, f_ref)


def edges_kernel(own_ref, xa_ref, xb_ref, xs_ref, ea_ref, eb_ref, fa_ref, fb_ref):
    cx, cy = own_ref.shape[:2]
    odd_x, odd_y = lax.axis_index(GX) & 1, lax.axis_index(GY) & 1
    to_rows(xa_ref, xs_ref.at[1 - odd_x], fa_ref)
    to_rows(xb_ref, xs_ref.at[odd_x], fb_ref)
    for edge_ref, first in ((ea_ref, (1 - odd_y) * (cy - 2)), (eb_ref, odd_y * (cy - 2))):
        edge_ref[0:2] = xs_ref[0, :, pl.ds(first, 2)]
        edge_ref[2 : 2 + cx] = own_ref[:, pl.ds(first, 2)]
        edge_ref[2 + cx : 4 + cx] = xs_ref[1, :, pl.ds(first, 2)]


def band_kernel(w_ref, o_ref):
    c = w_ref.shape[0]
    o_ref[...] = jnp.zeros_like(o_ref)
    for t in range(9):
        w = w_ref[:, t * 3 * c : (t + 1) * 3 * c]
        base = t * 6 * c
        o_ref[0:c, base : base + 2 * c] = w[:, c:]
        o_ref[0:c, base + 5 * c : base + 6 * c] = w[:, :c]
        for k in range(1, PACK):
            first = base + (k - 1) * c
            o_ref[k * c : (k + 1) * c, first : first + 3 * c] = w


def widen(f_ref, x_ref):
    rows = x_ref.shape[2]
    x_ref[:, :, :, 0:256] = f_ref[:, :, 8 : 8 + rows, :].astype(BF16)
    after = f_ref[:, :, 9 : 9 + rows, 0:128]
    before = f_ref[:, :, 7 : 7 + rows, 128:256]
    lane = lax.broadcasted_iota(jnp.int32, after.shape, 3)
    x_ref[:, :, :, 256:384] = jnp.where(lane < 64, after, before).astype(BF16)


def clear_ends(f_ref, rows):
    cells_x, cells_y, _, lanes = f_ref.shape
    zero = jnp.zeros((cells_x, cells_y, 1, lanes // 2), F32)
    f_ref[:, :, 7:8, lanes // 2 :] = zero
    f_ref[:, :, 8 + rows : 9 + rows, : lanes // 2] = zero


def banded_conv(x_ref, w_ref):
    nx, ny, rows, k = x_ref.shape
    nx, ny = nx - 2, ny - 2
    m = nx * ny * rows
    taps = [x_ref[dx : dx + nx, dy : dy + ny].reshape(m, k) for dx in range(3) for dy in range(3)]
    acc = None
    for first in range(0, 9, 2):
        last = min(first + 2, 9)
        part = lax.dot_general(
            jnp.concatenate(taps[first:last], axis=1),
            w_ref[:, first * k : last * k],
            (((1,), (1,)), ((), ())),
            preferred_element_type=F32,
        )
        acc = part if acc is None else acc + part
    return acc


def square_iota(n):
    return lax.broadcasted_iota(jnp.int32, (n, n), 0), lax.broadcasted_iota(jnp.int32, (n, n), 1)


def transposed(a):
    return jnp.transpose(a)


def split(a):
    high = a.astype(BF16)
    return high, (a - high.astype(F32)).astype(BF16)


def dot3(a, b):
    dot = functools.partial(jnp.dot, preferred_element_type=F32)
    a0, a1 = split(a)
    b0, b1 = split(b)
    return dot(a0, b0) + (dot(a0, b1) + dot(a1, b0))


def fold_blocks(wide):
    total = wide[0:64, 0:64]
    for k in range(1, PACK):
        total = total + wide[k * 64 : (k + 1) * 64, k * 64 : (k + 1) * 64]
    return total


def hidden_kernel(own_ref, xs_ref, yb_ref, ya_ref, w_ref, hidden_ref, pay_ref, f_ref, x_ref):
    rows = own_ref.shape[2]
    cx, cy = own_ref.shape[:2]
    clear_ends(f_ref, rows)
    f_ref[0:2, 2 : 2 + cy, 8 : 8 + rows, :] = xs_ref[0].astype(F32)
    f_ref[2 : 2 + cx, 2 : 2 + cy, 8 : 8 + rows, :] = own_ref[...].astype(F32)
    f_ref[2 + cx : 4 + cx, 2 : 2 + cy, 8 : 8 + rows, :] = xs_ref[1].astype(F32)
    odd_y = lax.axis_index(GY) & 1
    f_ref[:, pl.ds((1 - odd_y) * (cy + 2), 2), 8 : 8 + rows, :] = ya_ref[...].astype(F32)
    f_ref[:, pl.ds(odd_y * (cy + 2), 2), 8 : 8 + rows, :] = yb_ref[...].astype(F32)
    widen(f_ref, x_ref)
    hidden_ref[...] = banded_conv(x_ref, w_ref).reshape(hidden_ref.shape)
    own = hidden_ref[1 : 1 + cx, 1 : 1 + cy].reshape(cx * cy * rows, 256)
    sums = jnp.sum(own, axis=0, keepdims=True)
    total = sums[:, 0:64]
    for k in range(1, PACK):
        total = total + sums[:, k * 64 : (k + 1) * 64]
    cells = float(cx * cy * rows * PACK)
    high, low = split(own - jnp.concatenate([total / cells] * PACK, axis=1))
    outer = functools.partial(
        lax.dot_general, dimension_numbers=(((0,), (0,)), ((), ())), preferred_element_type=F32
    )
    mixed = fold_blocks(outer(high, low))
    i, j = square_iota(64)
    column = jnp.sum(jnp.where(i == j, total, 0.0), axis=1, keepdims=True)
    gram = fold_blocks(outer(high, high)) + (mixed + transposed(mixed)) + column * (total / cells)
    i, j = square_iota(32)
    low = gram[32:, 32:]
    tri = jnp.where(j >= i, gram[:32, :32], low)
    cross = gram[:32, 32:]
    block = jnp.concatenate([tri[:16], tri[16:], cross[:16], cross[16:]], axis=1)
    diag = jnp.sum(jnp.where(i == j, low, 0.0), axis=0, keepdims=True)
    last = jnp.concatenate([diag, total, jnp.zeros((1, 32), F32)], axis=1)
    for p in range(pay_ref.shape[0]):
        for r in range(16):
            pay_ref[p, r] = block[r : r + 1]
        pay_ref[p, 16] = last


def relay_kernel(in_ref, out_ref):
    total = jnp.sum(in_ref[...], axis=0)
    for p in range(out_ref.shape[0]):
        out_ref[p] = total


def moments(pay_ref, p_ref, count):
    total = jnp.sum(pay_ref[...], axis=0)
    for r in range(PAY):
        p_ref[r : r + 1, :] = total[r]
    block = p_ref[0:16, :]
    last = p_ref[16:17, :]
    i, j = square_iota(32)
    tri = jnp.concatenate([block[:, 0:32], block[:, 32:64]], axis=0)
    cross = jnp.concatenate([block[:, 64:96], block[:, 96:128]], axis=0)
    flip = transposed(tri)
    top = jnp.where(j >= i, tri, flip)
    low = jnp.where(j < i, tri, flip)
    low = jnp.where(i == j, jnp.broadcast_to(last[:, 0:32], (32, 32)), low)
    gram = jnp.concatenate(
        [
            jnp.concatenate([top, cross], axis=1),
            jnp.concatenate([transposed(cross), low], axis=1),
        ],
        axis=0,
    )
    mean = last[:, 32:96] / count
    i, j = square_iota(64)
    eye = jnp.where(i == j, 1.0, 0.0).astype(F32)
    column = jnp.sum(eye * mean, axis=1, keepdims=True)
    return mean, gram / count - column * mean + 1e-05 * eye, eye


def newton_whiten(sigma, eye):
    trace = jnp.sum(jnp.sum(sigma * eye, axis=1, keepdims=True), axis=0, keepdims=True)
    normed = sigma / trace
    proj = 1.5 * eye - 0.5 * normed
    for _ in range(NEWTON - 1):
        both = dot3(proj, jnp.concatenate([proj, normed], axis=1))
        proj = 1.5 * proj - 0.5 * dot3(both[:, 0:64], both[:, 64:128])
    return proj / jnp.sqrt(trace)


def output_kernel(
    pay_ref, hidden_ref, gain_ref, shift_ref, w_ref, bias_ref, out_ref, p_ref, f_ref, x_ref, o_ref, *, count
):
    nx, ny, rows, lanes = hidden_ref.shape
    mean, sigma, eye = moments(pay_ref, p_ref, count)
    whiten = newton_whiten(sigma, eye)
    i, j = square_iota(lanes)
    wide = jnp.concatenate([whiten] * PACK, axis=1)
    wide = jnp.concatenate([wide] * PACK, axis=0)
    wide = jnp.where(i >> 6 == j >> 6, wide, 0.0)
    mean = jnp.concatenate([mean] * PACK, axis=1)
    gain = jnp.concatenate([gain_ref[...]] * PACK, axis=1)
    shift = jnp.concatenate([shift_ref[...]] * PACK, axis=1)
    centered = hidden_ref[...].reshape(nx * ny * rows, lanes) - mean
    normalized = dot3(centered, wide)
    act = jnp.maximum(gain * normalized + shift, 0.0).reshape(hidden_ref.shape)
    clear_ends(f_ref, rows)
    f_ref[:, :, 8 : 8 + rows, :] = act
    at_x, at_y = lax.axis_index(GX), lax.axis_index(GY)
    for outside, edge in (
        (at_x == 0, f_ref.at[0]),
        (at_x == group_size(GX) - 1, f_ref.at[nx - 1]),
        (at_y == 0, f_ref.at[:, 0]),
        (at_y == group_size(GY) - 1, f_ref.at[:, ny - 1]),
    ):

        @pl.when(outside)
        def _(edge=edge):
            edge[...] = jnp.zeros_like(edge)

    widen(f_ref, x_ref)
    bias = jnp.concatenate([bias_ref[...]] * PACK, axis=1)
    result = banded_conv(x_ref, w_ref) + bias
    for h in range(lanes // 128):
        o_ref[h] = result[:, h * 128 : (h + 1) * 128]
    slabs, sub, _ = out_ref.shape
    for x in range(slabs):
        for b in range(rows):
            for h in range(lanes // 128):
                first = b * lanes + h * 128
                out_ref[x, :, first : first + 128] = o_ref[
                    h, pl.ds(x * sub * rows + b, sub, stride=rows), :
                ].astype(BF16)


def exchange(block, axes):
    return lax.all_to_all(block, axes, 0, 0, tiled=True)


def local(volume, conv_first, gain, shift, conv_second, bias_second):
    width = bias_second.shape[0]
    cx, cy, merged = volume.shape
    lanes = PACK * width
    rows = merged // lanes
    count = float(cx * group_size(GX) * cy * group_size(GY) * (merged // width))
    call = functools.partial(pl.pallas_call, compiler_params=params())
    xa, xb = swap(volume, GX, 0), swap(volume, GX, 1)
    block = jax.ShapeDtypeStruct((cx, cy, rows, lanes), BF16)
    half = pltpu.VMEM((lanes // 128, cx * cy * rows, 128), F32)
    own = call(rows_kernel, out_shape=block, scratch_shapes=[half], name="rows")(volume)
    band = call(band_kernel, out_shape=jax.ShapeDtypeStruct((lanes, 54 * width), BF16), name="band")
    first, second = band(conv_first.T), band(conv_second.T)
    xb, first, second = lax.optimization_barrier((xb, first, second))
    edge = jax.ShapeDtypeStruct((cx + 4, 2, rows, lanes), BF16)
    xs, ea, eb = call(
        edges_kernel,
        out_shape=(jax.ShapeDtypeStruct((2,) + block.shape, BF16), edge, edge),
        scratch_shapes=[half, half],
        name="edges",
    )(own, xa, xb)
    yb = swap(eb, GY, 1)
    ya = swap(ea, GY, 0)
    hidden, pay = call(
        hidden_kernel,
        out_shape=(
            jax.ShapeDtypeStruct((cx + 2, cy + 2, rows, lanes), F32),
            jax.ShapeDtypeStruct((group_size(GX[1:] + GY), PAY, 1, 128), F32),
        ),
        scratch_shapes=[
            pltpu.VMEM((cx + 4, cy + 4, rows + 16, lanes), F32),
            pltpu.VMEM((cx + 4, cy + 4, rows, 6 * width), BF16),
        ],
        name="hidden",
    )(own, xs, yb, ya, first)
    rest, line = GX[1:] + GY, GX[:1]
    pay = exchange(pay, rest)
    pay = call(
        relay_kernel, out_shape=jax.ShapeDtypeStruct((group_size(line), PAY, 1, 128), F32), name="relay"
    )(pay)
    pay = exchange(pay, line)
    return call(
        functools.partial(output_kernel, count=count),
        out_shape=jax.ShapeDtypeStruct((cx, cy, merged), BF16),
        scratch_shapes=[
            pltpu.VMEM((24, 128), F32),
            pltpu.VMEM((cx + 2, cy + 2, rows + 16, lanes), F32),
            pltpu.VMEM((cx + 2, cy + 2, rows, 6 * width), BF16),
            pltpu.VMEM((lanes // 128, cx * cy * rows, 128), F32),
        ],
        name="output",
    )(pay, hidden, gain[None], shift[None], second, bias_second[None])


def solution(mesh):
    torus = Mesh(mesh.devices.reshape(16, 4, 4, 2), GX + GY)
    placed = (P(GX, GY, None), P(), P(), P(), P(), P())
    return jax.shard_map(
        local, mesh=torus, in_specs=placed, out_specs=P(GX, GY, None), check_vma=False
    )
```
